32 devices in a mesh: groups: 2 (over y), ctx: 16 (over z, x, core).
Axes of the slice: x: 2, y: 2, z: 4, core: 2. Of those that a mesh axis runs over, the one named last changes fastest.
Arguments:
- queries: bfloat16 [32, 8192], P(('groups', 'ctx')), parts along dimension 0, may hold values from -120 to 120
- fresh_keys: bfloat16 [32, 512], P(('groups', 'ctx')), parts along dimension 0, may hold values from -4 to 4
- fresh_values: bfloat16 [32, 512], P(('groups', 'ctx')), parts along dimension 0, may hold values from -4 to 4
- cache_keys: bfloat16 [32768, 512], P(('groups', 'ctx')), parts along dimension 0, may hold values from -4 to 4
- stored_values: bfloat16 [32768, 512], P(('groups', 'ctx')), parts along dimension 0, may hold values from -4 to 4
- cache_lengths: int32 [32], P(('groups', 'ctx')), parts along dimension 0, may hold values from 1 to 1024, as said below
- positions: int32 [32], P('groups'), parts along dimension 0, may hold values from 0 to 15, each once
Outputs:
- attended: bfloat16 [32, 8192], P(('groups', 'ctx')), parts along dimension 0
The draws below stay inside these ranges and needn't reach their ends.
There are 2 independent parts, one for each index of `groups`. The reference program is written for one: setup_inputs(seed, part) draws one part's arguments, and reference() takes and returns one part's arrays. A program takes and returns all parts, laid end to end along the dimension named above; each array names one. Nothing has to cross between parts.
Inputs may be any that keep to these rules, and one draw needn't show every extreme that they name: `cache_lengths`: each entry lies between 1 and 1024, and one shard has all 1024 slots live.
All inputs are finite; a program needn't handle non-finite values.
Results may differ from the reference program's by a relative error of at most 0.003.
Values may be sent and summed in bfloat16 or wider, within the bound.
A program may use at most 128 MiB of HBM per device.

```python
import jax
import jax.numpy as jnp
from jax import lax

KEY_VALUE_HEADS = 4
HEADS_PER_GROUP = 16
HEAD_WIDTH = 128
QUERY_HEADS = 64
NEW_DEV = 1
CACHE_DEV = 1024
NEW_TOKENS = 16
CACHE_SLOTS = 16384
N_CTX = 16


def full_shard(key):
    return jax.random.randint(jax.random.fold_in(key, 7), (), 0, N_CTX)


def key_table(key):
    return jnp.clip(jax.random.normal(jax.random.fold_in(key, 21), (CACHE_SLOTS, KEY_VALUE_HEADS * HEAD_WIDTH), jnp.float32), -4.0, 4.0)


def draw_cache_lengths(key, part):
    first = jax.random.randint(jax.random.fold_in(key, 11), (N_CTX,), 1, CACHE_DEV + 1)
    second = jax.random.randint(jax.random.fold_in(key, 12), (N_CTX,), 1, CACHE_DEV + 1)
    lengths = jnp.maximum(first * second // CACHE_DEV, 1)
    lengths = jnp.where(jnp.arange(N_CTX) == full_shard(key), CACHE_DEV, lengths)
    return lengths.astype(jnp.int32)


def draw_cache_keys(key, part):
    lookup_table = key_table(key)
    return lookup_table.astype(jnp.bfloat16)


def draw_queries(key, part):
    base = 2.5 * jnp.clip(jax.random.normal(jax.random.fold_in(key, 31), (NEW_TOKENS, QUERY_HEADS * HEAD_WIDTH), jnp.float32), -4.0, 4.0)
    return base.astype(jnp.bfloat16)


def block_levels(stream_key, extent, split, low, high):
    loudness, own = 1.0, jax.random.fold_in(stream_key, 6)
    for position, shards_of in split:
        draws = jnp.exp(jax.random.uniform(jax.random.fold_in(own, position), (shards_of,), jnp.float32, low / len(split), high / len(split)))
        loudness = loudness * jnp.repeat(draws, extent[position] // shards_of).reshape([-1 if axis == position else 1 for axis in range(len(extent))])
    return loudness


def centred(stream_key, dims, deviation, limit, pieces=(), kind=jnp.bfloat16):
    drawn = deviation * jax.random.normal(stream_key, dims, jnp.float32)
    if pieces:
        drawn = drawn * block_levels(stream_key, dims, pieces, -0.22, 0.18)
    return jnp.clip(drawn, -limit, limit).astype(kind)


def setup_inputs(seed: int = 0, part: int = 0) -> dict:
    key_list = jax.random.split(jax.random.key(seed), 8)
    part_keys = jax.random.split(jax.random.fold_in(key_list[7], part), 8)
    return {
        "queries": draw_queries(jax.random.fold_in(jax.random.fold_in(key_list[7], part), 71), part),
        "fresh_keys": centred(part_keys[1], (NEW_TOKENS, KEY_VALUE_HEADS * HEAD_WIDTH), 1.0, 4.0, ((0, 16),)),
        "fresh_values": centred(part_keys[2], (NEW_TOKENS, KEY_VALUE_HEADS * HEAD_WIDTH), 1.0, 4.0, ((0, 16),)),
        "cache_keys": draw_cache_keys(jax.random.fold_in(jax.random.fold_in(key_list[7], part), 71), part),
        "stored_values": centred(part_keys[4], (CACHE_SLOTS, KEY_VALUE_HEADS * HEAD_WIDTH), 1.0, 4.0, ((0, 16),)),
        "cache_lengths": draw_cache_lengths(jax.random.fold_in(jax.random.fold_in(key_list[7], part), 71), part),
        "positions": jax.random.permutation(part_keys[6], NEW_TOKENS).astype(jnp.int32),
    }


def block_partials(queries, keys_of_block, values_of_block, visible):
    slice_width = keys_of_block.shape[0]
    query_float = queries.astype(jnp.float32).reshape(NEW_TOKENS, KEY_VALUE_HEADS, HEADS_PER_GROUP, HEAD_WIDTH)
    key_float = keys_of_block.astype(jnp.float32).reshape(slice_width, KEY_VALUE_HEADS, HEAD_WIDTH)
    value_float = values_of_block.astype(jnp.float32).reshape(slice_width, KEY_VALUE_HEADS, HEAD_WIDTH)
    scores = jnp.einsum("nhgd,khd->nhgk", query_float, key_float) * (HEAD_WIDTH ** -0.5)
    scores = jnp.where(visible[:, None, None, :], scores, -jnp.inf)
    maxima = jnp.max(scores, axis=-1)
    weights = jnp.exp(scores - maxima[..., None]).astype(jnp.bfloat16)
    totals = jnp.sum(weights.astype(jnp.float32), axis=-1)
    sums = jnp.einsum("nhgk,khd->nhgd", weights.astype(jnp.float32), value_float)
    return maxima.reshape(NEW_TOKENS, QUERY_HEADS), totals.reshape(NEW_TOKENS, QUERY_HEADS), sums.reshape(NEW_TOKENS, QUERY_HEADS, HEAD_WIDTH)


def reference(queries, fresh_keys, fresh_values, cache_keys, stored_values, cache_lengths, positions):
    def step(carry, block):
        run_max, run_sum, run_total = carry
        first = (block * CACHE_DEV).astype(jnp.int32)
        second = (block * NEW_DEV).astype(jnp.int32)
        keys_of_block = jnp.concatenate([lax.dynamic_slice_in_dim(cache_keys, first, CACHE_DEV, 0), lax.dynamic_slice_in_dim(fresh_keys, second, NEW_DEV, 0)], axis=0)
        values_of_block = jnp.concatenate([lax.dynamic_slice_in_dim(stored_values, first, CACHE_DEV, 0), lax.dynamic_slice_in_dim(fresh_values, second, NEW_DEV, 0)], axis=0)
        key_order = lax.dynamic_slice_in_dim(positions, second, NEW_DEV, 0)
        live = jnp.arange(CACHE_DEV, dtype=jnp.int32) < cache_lengths[block]
        cache_seen = jnp.broadcast_to(live[None, :], (NEW_TOKENS, CACHE_DEV))
        new_seen = key_order[None, :] <= positions[:, None]
        visible = jnp.concatenate([cache_seen, new_seen], axis=1)
        maxima, totals, sums = block_partials(queries, keys_of_block, values_of_block, visible)
        top = jnp.maximum(run_max, maxima)
        old_scale = jnp.exp(run_max - top)
        new_scale = jnp.exp(maxima - top)
        run_sum = run_sum * old_scale[..., None] + sums * new_scale[..., None]
        run_total = run_total * old_scale + totals * new_scale
        return (top, run_sum, run_total), None

    start = (jnp.full((NEW_TOKENS, QUERY_HEADS), -jnp.inf, jnp.float32), jnp.zeros((NEW_TOKENS, QUERY_HEADS, HEAD_WIDTH), jnp.float32), jnp.zeros((NEW_TOKENS, QUERY_HEADS), jnp.float32))
    (run_max, run_sum, run_total), unused = lax.scan(step, start, jnp.arange(N_CTX, dtype=jnp.int32))
    result = run_sum / run_total[..., None]
    return result.reshape(NEW_TOKENS, QUERY_HEADS * HEAD_WIDTH).astype(jnp.bfloat16)
```

```python
import functools
import math

import jax
import jax.numpy as jnp
from jax import lax
from jax.experimental import pallas as pl
from jax.experimental.pallas import tpu as pltpu
from jax.sharding import PartitionSpec as P

HEADS_PER_GROUP = 16
HEAD_WIDTH = 128
MESH = pl.DeviceIdType.MESH


def partner(rank, step, count):
    if count & (count - 1) == 0:
        return rank ^ step
    return lax.rem(rank + step, count)


def source(rank, step, count):
    if count & (count - 1) == 0:
        return rank ^ step
    return lax.rem(rank + count - step, count)


def kernel(n, chunk, lengths_ref, positions_ref, q_ref, fk_ref, fv_ref, keys_hbm, values_hbm, out_ref,
           keys, values, q_all, sums, stats, sums_in, stats_in,
           kv_sem, q_send, q_recv, s_send, s_recv, t_send, t_recv):
    me = lax.axis_index("ctx")
    cache_rows = keys.shape[0]
    heads = q_ref.shape[0]
    width = HEAD_WIDTH
    group = HEADS_PER_GROUP
    kv_heads = heads // group
    factor = width ** -0.5 * math.log2(math.e)

    key_copy = pltpu.make_async_copy(keys_hbm, keys, kv_sem.at[0])
    value_copy = pltpu.make_async_copy(values_hbm, values, kv_sem.at[1])
    key_copy.start()
    value_copy.start()

    barrier = pltpu.get_barrier_semaphore()

    @pl.loop(1, n)
    def _(step):
        pl.semaphore_signal(barrier, inc=1, device_id={"ctx": partner(me, step, n)}, device_id_type=MESH)

    pl.semaphore_wait(barrier, n - 1)

    def q_copy(peer):
        return pltpu.make_async_remote_copy(
            src_ref=q_ref, dst_ref=q_all.at[me], send_sem=q_send.at[peer], recv_sem=q_recv.at[me],
            device_id={"ctx": peer}, device_id_type=MESH)

    def q_arrival(peer):
        return pltpu.make_async_remote_copy(
            src_ref=q_ref, dst_ref=q_all.at[peer], send_sem=q_send.at[peer], recv_sem=q_recv.at[peer],
            device_id={"ctx": peer}, device_id_type=MESH)

    @pl.loop(1, n)
    def _(step):
        q_copy(partner(me, n - step, n)).start()

    q_all[me] = q_ref[...]

    key_copy.wait()
    value_copy.wait()

    dead = jnp.where(
        lax.broadcasted_iota(jnp.int32, (1, cache_rows), 1) < lengths_ref[0], 0.0, -jnp.inf
    ).astype(jnp.float32)
    lane = lax.broadcasted_iota(jnp.int32, (group, width), 1)
    row = lax.broadcasted_iota(jnp.int32, (group, width), 0)
    ones = jnp.ones((cache_rows, width), jnp.bfloat16)
    own_order = positions_ref[me]
    n_chunks = n // chunk
    my_chunk = me // chunk

    def sums_copy(peer):
        return pltpu.make_async_remote_copy(
            src_ref=sums.at[peer], dst_ref=sums_in.at[me], send_sem=s_send.at[peer], recv_sem=s_recv.at[me],
            device_id={"ctx": peer}, device_id_type=MESH)

    def stats_copy(peer):
        return pltpu.make_async_remote_copy(
            src_ref=stats.at[peer], dst_ref=stats_in.at[me], send_sem=t_send.at[peer], recv_sem=t_recv.at[me],
            device_id={"ctx": peer}, device_id_type=MESH)

    def process(base):
        fresh_bias = jnp.concatenate(
            [jnp.full((group, 1), jnp.where(own_order <= positions_ref[base + i], 0.0, -jnp.inf), jnp.float32)
             for i in range(chunk)], axis=0)
        packed = [jnp.zeros((group, width), jnp.float32) for _ in range(chunk)]
        for h in range(kv_heads):
            cols = slice(h * width, (h + 1) * width)
            q = q_all[pl.ds(base, chunk), h * group:(h + 1) * group, :].reshape(chunk * group, width)
            s = lax.dot_general(q, keys[:, cols], (((1,), (1,)), ((), ())),
                                preferred_element_type=jnp.float32) + dead
            fk = fk_ref[:, cols].astype(jnp.float32)
            fv = fv_ref[:, cols].astype(jnp.float32)
            sf = jnp.sum(q.astype(jnp.float32) * fk, axis=1, keepdims=True) + fresh_bias
            m = jnp.maximum(jnp.max(s, axis=1, keepdims=True), sf)
            p = jnp.exp2((s - m) * factor).astype(jnp.bfloat16)
            pf = jnp.exp2((sf - m) * factor).astype(jnp.bfloat16).astype(jnp.float32)
            o = jnp.dot(p, jnp.concatenate([values[:, cols], ones], axis=1), preferred_element_type=jnp.float32)
            total = o[:, width:] + pf
            block = o[:, :width] + pf * fv
            sums[pl.ds(base, chunk), h * group:(h + 1) * group, :] = block.astype(jnp.bfloat16).reshape(
                chunk, group, width)
            for i in range(chunk):
                part = slice(i * group, (i + 1) * group)
                packed[i] = jnp.where(lane == row + h * group, m[part], packed[i])
                packed[i] = jnp.where(lane == row + h * group + heads, total[part], packed[i])
        for i in range(chunk):
            stats[base + i] = jnp.sum(packed[i], axis=0, keepdims=True)

    @pl.loop(0, n_chunks)
    def _(step):
        base = source(my_chunk, step, n_chunks) * chunk

        @pl.loop(0, chunk)
        def _(i):
            @pl.when(base + i != me)
            def _():
                q_arrival(base + i).wait_recv()

        process(base)

        @pl.loop(0, chunk)
        def _(i):
            @pl.when(base + i != me)
            def _():
                stats_copy(base + i).start()
                sums_copy(base + i).start()

    stats_in[me] = stats[me]
    sums_in[me] = sums[me]

    @pl.loop(1, n)
    def _(step):
        peer = partner(me, step, n)
        pltpu.make_async_remote_copy(
            src_ref=stats.at[peer], dst_ref=stats_in.at[peer], send_sem=t_send.at[peer], recv_sem=t_recv.at[peer],
            device_id={"ctx": peer}, device_id_type=MESH).wait_recv()

    st = stats_in[...].reshape(n, width)
    coef = jnp.exp2((st - jnp.max(st, axis=0, keepdims=True)) * factor)
    den = jnp.sum(coef * pltpu.roll(st, width - heads, 1), axis=0, keepdims=True)
    w = coef / den
    if n < width:
        w = jnp.concatenate([w, jnp.zeros((width - n, width), jnp.float32)], axis=0)
    w = w.T

    @pl.loop(1, n)
    def _(step):
        peer = partner(me, step, n)
        pltpu.make_async_remote_copy(
            src_ref=sums.at[peer], dst_ref=sums_in.at[peer], send_sem=s_send.at[peer], recv_sem=s_recv.at[peer],
            device_id={"ctx": peer}, device_id_type=MESH).wait_recv()

    result = jnp.zeros((heads, width), jnp.float32)
    for b in range(n):
        result += w[:heads, b:b + 1] * sums_in[b].astype(jnp.float32)
    out_ref[...] = result.astype(jnp.bfloat16)

    @pl.loop(1, n)
    def _(step):
        peer = partner(me, step, n)
        q_copy(peer).wait_send()
        stats_copy(peer).wait_send()
        sums_copy(peer).wait_send()


def body(n, queries, fresh_keys, fresh_values, cache_keys, stored_values, cache_lengths, positions):
    rows = queries.shape[0]
    assert rows == 1
    heads = queries.shape[1] // HEAD_WIDTH
    cache_rows, kv_width = cache_keys.shape
    vmem = pl.BlockSpec(memory_space=pltpu.VMEM)
    smem = pl.BlockSpec(memory_space=pltpu.SMEM)
    hbm = pl.BlockSpec(memory_space=pl.ANY)
    chunk = 4 if n % 4 == 0 else 1
    block = (n, heads, HEAD_WIDTH)
    dma = pltpu.SemaphoreType.DMA
    out = pl.pallas_call(
        functools.partial(kernel, n, chunk),
        out_shape=jax.ShapeDtypeStruct((heads, HEAD_WIDTH), jnp.bfloat16),
        in_specs=[smem, smem, vmem, vmem, vmem, hbm, hbm],
        out_specs=vmem,
        scratch_shapes=[
            pltpu.VMEM((cache_rows, kv_width), jnp.bfloat16),
            pltpu.VMEM((cache_rows, kv_width), jnp.bfloat16),
            pltpu.VMEM(block, jnp.bfloat16),
            pltpu.VMEM(block, jnp.bfloat16),
            pltpu.VMEM((n, 1, HEAD_WIDTH), jnp.float32),
            pltpu.VMEM(block, jnp.bfloat16),
            pltpu.VMEM((n, 1, HEAD_WIDTH), jnp.float32),
            dma((2,)), dma((n,)), dma((n,)), dma((n,)), dma((n,)), dma((n,)), dma((n,)),
        ],
        compiler_params=pltpu.CompilerParams(collective_id=0, has_side_effects=True),
    )(cache_lengths, positions, queries.reshape(heads, HEAD_WIDTH), fresh_keys, fresh_values,
      cache_keys, stored_values)
    return out.reshape(rows, heads * HEAD_WIDTH)


def solution(mesh):
    return jax.shard_map(
        functools.partial(body, mesh.shape["ctx"]),
        mesh=mesh,
        in_specs=(
            P(("groups", "ctx"), None),
            P(("groups", "ctx"), None),
            P(("groups", "ctx"), None),
            P(("groups", "ctx"), None),
            P(("groups", "ctx"), None),
            P(("groups", "ctx")),
            P("groups"),
        ),
        out_specs=P(("groups", "ctx"), None),
        check_vma=False,
    )
```

```python
import functools
import math

import jax
import jax.numpy as jnp
from jax import lax
from jax.experimental import pallas as pl
from jax.experimental.pallas import tpu as pltpu
from jax.sharding import PartitionSpec as P

HEADS_PER_GROUP = 16
HEAD_WIDTH = 128
MESH = pl.DeviceIdType.MESH


def kernel(n, chunk, queries_hbm, fresh_keys_hbm, fresh_values_hbm, keys_hbm, values_hbm, lengths_hbm, positions_hbm,
           out_ref, keys, values, q_row, fk_ref, fv_ref, lengths_ref, positions_ref,
           q_all, sums, stats, sums_in, stats_in,
           load_sem, q_send, q_recv, s_send, s_recv, t_send, t_recv):
    me = lax.axis_index("ctx")
    cache_rows = keys.shape[0]
    heads = q_all.shape[1]
    width = HEAD_WIDTH
    group = HEADS_PER_GROUP
    kv_heads = heads // group
    factor = width ** -0.5 * math.log2(math.e)
    line = n // chunk
    beside, across = me ^ 1, me ^ 2

    loads = [
        pltpu.make_async_copy(src, dst, load_sem.at[i])
        for i, (src, dst) in enumerate([
            (queries_hbm, q_row), (keys_hbm, keys), (values_hbm, values), (fresh_keys_hbm, fk_ref),
            (fresh_values_hbm, fv_ref), (lengths_hbm, lengths_ref), (positions_hbm, positions_ref)])
    ]
    for load in loads:
        load.start()

    barrier = pltpu.get_barrier_semaphore()
    pl.semaphore_signal(barrier, inc=1, device_id={"ctx": beside}, device_id_type=MESH)
    pl.semaphore_signal(barrier, inc=1, device_id={"ctx": across}, device_id_type=MESH)

    @pl.loop(1, line)
    def _(t):
        pl.semaphore_signal(barrier, inc=1, device_id={"ctx": me ^ (t * chunk)}, device_id_type=MESH)

    loads[0].wait()
    q_all[me] = q_row[...].astype(jnp.float32).reshape(heads, width).astype(jnp.bfloat16)
    pl.semaphore_wait(barrier, line + 1)

    def q_copy(row, peer, slot):
        return pltpu.make_async_remote_copy(
            src_ref=q_all.at[row], dst_ref=q_all.at[row], send_sem=q_send.at[slot], recv_sem=q_recv.at[row],
            device_id={"ctx": peer}, device_id_type=MESH)

    def to_line(t):
        return q_copy(me, me ^ (t * chunk), t)

    def to_across(t):
        return q_copy(me ^ (t * chunk), across, line + t)

    def to_beside(t, far):
        return q_copy((across if far else me) ^ (t * chunk), beside, (2 + far) * line + t)

    def arrive(row):
        q_copy(row, beside, 0).wait_recv()

    @pl.loop(1, line)
    def _(t):
        to_line(line - t).start()

    to_across(0).start()
    to_beside(0, 0).start()

    @pl.loop(1, line)
    def _(t):
        arrive(me ^ (t * chunk))
        to_across(t).start()
        to_beside(t, 0).start()
        arrive(across ^ ((t - 1) * chunk))
        to_beside(t - 1, 1).start()

    def last_across():
        arrive(across ^ ((line - 1) * chunk))
        to_beside(line - 1, 1).start()

    for load in loads[1:]:
        load.wait()

    dead = jnp.where(
        lax.broadcasted_iota(jnp.int32, (1, cache_rows), 1) < lengths_ref[0], 0.0, -jnp.inf
    ).astype(jnp.float32)
    lane = lax.broadcasted_iota(jnp.int32, (group, width), 1)
    row = lax.broadcasted_iota(jnp.int32, (group, width), 0)
    ones = jnp.ones((cache_rows, width), jnp.bfloat16)
    own_order = positions_ref[me]
    if line == 1:
        last_across()

    def sums_copy(peer):
        return pltpu.make_async_remote_copy(
            src_ref=sums.at[peer], dst_ref=sums_in.at[me], send_sem=s_send.at[peer], recv_sem=s_recv.at[me],
            device_id={"ctx": peer}, device_id_type=MESH)

    def stats_copy(peer):
        return pltpu.make_async_remote_copy(
            src_ref=stats.at[peer], dst_ref=stats_in.at[me], send_sem=t_send.at[peer], recv_sem=t_recv.at[me],
            device_id={"ctx": peer}, device_id_type=MESH)

    def process(base):
        fresh_bias = jnp.concatenate(
            [jnp.full((group, 1), jnp.where(own_order <= positions_ref[base + i], 0.0, -jnp.inf), jnp.float32)
             for i in range(chunk)], axis=0)
        packed = [jnp.zeros((group, width), jnp.float32) for _ in range(chunk)]
        for h in range(kv_heads):
            cols = slice(h * width, (h + 1) * width)
            q = q_all[pl.ds(base, chunk), h * group:(h + 1) * group, :].reshape(chunk * group, width)
            s = lax.dot_general(q, keys[:, cols], (((1,), (1,)), ((), ())),
                                preferred_element_type=jnp.float32) + dead
            fk = fk_ref[:, cols].astype(jnp.float32)
            fv = fv_ref[:, cols].astype(jnp.float32)
            sf = jnp.sum(q.astype(jnp.float32) * fk, axis=1, keepdims=True) + fresh_bias
            m = jnp.maximum(jnp.max(s, axis=1, keepdims=True), sf)
            p = jnp.exp2((s - m) * factor).astype(jnp.bfloat16)
            pf = jnp.exp2((sf - m) * factor).astype(jnp.bfloat16).astype(jnp.float32)
            o = jnp.dot(p, jnp.concatenate([values[:, cols], ones], axis=1), preferred_element_type=jnp.float32)
            total = o[:, width:] + pf
            block = (o[:, :width] + pf * fv) / total
            sums[pl.ds(base, chunk), h * group:(h + 1) * group, :] = block.astype(jnp.bfloat16).reshape(
                chunk, group, width)
            for i in range(chunk):
                part = slice(i * group, (i + 1) * group)
                packed[i] = jnp.where(lane == row + h * group, m[part], packed[i])
                packed[i] = jnp.where(lane == row + h * group + heads, total[part], packed[i])
        for i in range(chunk):
            stats[base + i] = jnp.sum(packed[i], axis=0, keepdims=True)

    @pl.loop(0, line)
    def _(step):
        base = (me ^ (step * chunk)) // chunk * chunk

        @pl.when(step == 1)
        def _():
            last_across()

        arrive(beside ^ (step * chunk))
        arrive(beside ^ 2 ^ (step * chunk))
        process(base)

        @pl.loop(0, chunk)
        def _(i):
            @pl.when(base + i != me)
            def _():
                stats_copy(base + i).start()
                sums_copy(base + i).start()

    stats_in[me] = stats[me]
    sums_in[me] = sums[me]

    @pl.loop(1, n)
    def _(step):
        peer = me ^ step
        pltpu.make_async_remote_copy(
            src_ref=stats.at[peer], dst_ref=stats_in.at[peer], send_sem=t_send.at[peer], recv_sem=t_recv.at[peer],
            device_id={"ctx": peer}, device_id_type=MESH).wait_recv()

    st = stats_in[...].reshape(n, width)
    coef = jnp.exp2((st - jnp.max(st, axis=0, keepdims=True)) * factor) * pltpu.roll(st, width - heads, 1)
    w = coef / jnp.sum(coef, axis=0, keepdims=True)
    if n < width:
        w = jnp.concatenate([w, jnp.zeros((width - n, width), jnp.float32)], axis=0)
    w = w.T

    @pl.loop(1, n)
    def _(step):
        peer = me ^ step
        pltpu.make_async_remote_copy(
            src_ref=sums.at[peer], dst_ref=sums_in.at[peer], send_sem=s_send.at[peer], recv_sem=s_recv.at[peer],
            device_id={"ctx": peer}, device_id_type=MESH).wait_recv()

    result = jnp.zeros((heads, width), jnp.float32)
    for b in range(n):
        result += w[:heads, b:b + 1] * sums_in[b].astype(jnp.float32)
    out_ref[...] = result.astype(jnp.bfloat16)

    @pl.loop(1, n)
    def _(step):
        peer = me ^ step
        stats_copy(peer).wait_send()
        sums_copy(peer).wait_send()

    @pl.loop(1, n)
    def _(slot):
        q_copy(me, beside, slot).wait_send()


def body(n, queries, fresh_keys, fresh_values, cache_keys, stored_values, cache_lengths, positions):
    rows = queries.shape[0]
    assert rows == 1
    heads = queries.shape[1] // HEAD_WIDTH
    cache_rows, kv_width = cache_keys.shape
    chunk = 4
    assert n & (n - 1) == 0 and n % chunk == 0 and 2 * heads <= HEAD_WIDTH
    block = (n, heads, HEAD_WIDTH)
    operands = (queries, fresh_keys, fresh_values, cache_keys, stored_values, cache_lengths, positions)
    dma = pltpu.SemaphoreType.DMA
    out = pl.pallas_call(
        functools.partial(kernel, n, chunk),
        out_shape=jax.ShapeDtypeStruct((heads, HEAD_WIDTH), jnp.bfloat16),
        in_specs=[pl.BlockSpec(memory_space=pl.ANY)] * len(operands),
        out_specs=pl.BlockSpec(memory_space=pltpu.VMEM),
        scratch_shapes=[
            pltpu.VMEM((cache_rows, kv_width), jnp.bfloat16),
            pltpu.VMEM((cache_rows, kv_width), jnp.bfloat16),
            pltpu.VMEM(queries.shape, jnp.bfloat16),
            pltpu.VMEM(fresh_keys.shape, jnp.bfloat16),
            pltpu.VMEM(fresh_values.shape, jnp.bfloat16),
            pltpu.SMEM(cache_lengths.shape, jnp.int32),
            pltpu.SMEM(positions.shape, jnp.int32),
            pltpu.VMEM(block, jnp.bfloat16),
            pltpu.VMEM(block, jnp.bfloat16),
            pltpu.VMEM((n, 1, HEAD_WIDTH), jnp.float32),
            pltpu.VMEM(block, jnp.bfloat16),
            pltpu.VMEM((n, 1, HEAD_WIDTH), jnp.float32),
            dma((len(operands),)), dma((n,)), dma((n,)), dma((n,)), dma((n,)), dma((n,)), dma((n,)),
        ],
        compiler_params=pltpu.CompilerParams(collective_id=0, has_side_effects=True),
    )(*operands)
    return out.reshape(rows, heads * HEAD_WIDTH)


def solution(mesh):
    return jax.shard_map(
        functools.partial(body, mesh.shape["ctx"]),
        mesh=mesh,
        in_specs=(
            P(("groups", "ctx"), None),
            P(("groups", "ctx"), None),
            P(("groups", "ctx"), None),
            P(("groups", "ctx"), None),
            P(("groups", "ctx"), None),
            P(("groups", "ctx")),
            P("groups"),
        ),
        out_specs=P(("groups", "ctx"), None),
        check_vma=False,
    )
```

```python
import functools
import math

import jax
import jax.numpy as jnp
from jax import lax
from jax.experimental import pallas as pl
from jax.experimental.pallas import tpu as pltpu
from jax.sharding import PartitionSpec as P

HEADS_PER_GROUP = 16
HEAD_WIDTH = 128
MESH = pl.DeviceIdType.MESH


def kernel(n, chunk, queries_hbm, fresh_keys_hbm, fresh_values_hbm, keys_hbm, values_hbm, lengths_hbm, positions_hbm,
           out_ref, keys, values, q_row, fk_ref, fv_ref, lengths_ref, positions_ref,
           q_all, sums, stats, sums_in, stats_in,
           load_sem, q_send, q_recv, s_send, s_recv, t_send, t_recv):
    me = lax.axis_index("ctx")
    cache_rows = keys.shape[0]
    heads = q_all.shape[1]
    width = HEAD_WIDTH
    group = HEADS_PER_GROUP
    kv_heads = heads // group
    factor = width ** -0.5 * math.log2(math.e)
    line = n // chunk

    loads = [
        pltpu.make_async_copy(src, dst, load_sem.at[i])
        for i, (src, dst) in enumerate([
            (queries_hbm, q_row), (keys_hbm, keys), (values_hbm, values), (fresh_keys_hbm, fk_ref),
            (fresh_values_hbm, fv_ref), (lengths_hbm, lengths_ref), (positions_hbm, positions_ref)])
    ]
    for load in loads:
        load.start()

    barrier = pltpu.get_barrier_semaphore()

    @pl.loop(1, n)
    def _(step):
        pl.semaphore_signal(barrier, inc=1, device_id={"ctx": me ^ step}, device_id_type=MESH)

    loads[0].wait()
    q_all[me] = q_row[...].astype(jnp.float32).reshape(heads, width).astype(jnp.bfloat16)
    pl.semaphore_wait(barrier, n - 1)

    def q_copy(row, peer):
        return pltpu.make_async_remote_copy(
            src_ref=q_all.at[row], dst_ref=q_all.at[row], send_sem=q_send.at[peer], recv_sem=q_recv.at[row],
            device_id={"ctx": peer}, device_id_type=MESH)

    @pl.loop(1, n)
    def _(step):
        q_copy(me, me ^ step).start()

    for load in loads[1:]:
        load.wait()

    dead = jnp.where(
        lax.broadcasted_iota(jnp.int32, (1, cache_rows), 1) < lengths_ref[0], 0.0, -jnp.inf
    ).astype(jnp.float32)
    lane = lax.broadcasted_iota(jnp.int32, (group, width), 1)
    row = lax.broadcasted_iota(jnp.int32, (group, width), 0)
    ones = jnp.ones((cache_rows, width), jnp.bfloat16)
    own_order = positions_ref[me]

    def sums_copy(peer):
        return pltpu.make_async_remote_copy(
            src_ref=sums.at[peer], dst_ref=sums_in.at[me], send_sem=s_send.at[peer], recv_sem=s_recv.at[me],
            device_id={"ctx": peer}, device_id_type=MESH)

    def stats_copy(peer):
        return pltpu.make_async_remote_copy(
            src_ref=stats.at[peer], dst_ref=stats_in.at[me], send_sem=t_send.at[peer], recv_sem=t_recv.at[me],
            device_id={"ctx": peer}, device_id_type=MESH)

    def process(base):
        fresh_bias = jnp.concatenate(
            [jnp.full((group, 1), jnp.where(own_order <= positions_ref[base + i], 0.0, -jnp.inf), jnp.float32)
             for i in range(chunk)], axis=0)
        packed = [jnp.zeros((group, width), jnp.float32) for _ in range(chunk)]
        for h in range(kv_heads):
            cols = slice(h * width, (h + 1) * width)
            q = q_all[pl.ds(base, chunk), h * group:(h + 1) * group, :].reshape(chunk * group, width)
            s = lax.dot_general(q, keys[:, cols], (((1,), (1,)), ((), ())),
                                preferred_element_type=jnp.float32) + dead
            fk = fk_ref[:, cols].astype(jnp.float32)
            fv = fv_ref[:, cols].astype(jnp.float32)
            sf = jnp.sum(q.astype(jnp.float32) * fk, axis=1, keepdims=True) + fresh_bias
            m = jnp.maximum(jnp.max(s, axis=1, keepdims=True), sf)
            p = jnp.exp2((s - m) * factor).astype(jnp.bfloat16)
            pf = jnp.exp2((sf - m) * factor).astype(jnp.bfloat16).astype(jnp.float32)
            o = jnp.dot(p, jnp.concatenate([values[:, cols], ones], axis=1), preferred_element_type=jnp.float32)
            total = o[:, width:] + pf
            block = (o[:, :width] + pf * fv) / total
            sums[pl.ds(base, chunk), h * group:(h + 1) * group, :] = block.astype(jnp.bfloat16).reshape(
                chunk, group, width)
            for i in range(chunk):
                part = slice(i * group, (i + 1) * group)
                packed[i] = jnp.where(lane == row + h * group, m[part], packed[i])
                packed[i] = jnp.where(lane == row + h * group + heads, total[part], packed[i])
        for i in range(chunk):
            stats[base + i] = jnp.sum(packed[i], axis=0, keepdims=True)

    @pl.loop(0, line)
    def _(step):
        base = (me ^ (step * chunk)) // chunk * chunk

        @pl.loop(0, chunk)
        def _(i):
            @pl.when(base + i != me)
            def _():
                q_copy(base + i, base + i).wait_recv()

        process(base)

        @pl.loop(0, chunk)
        def _(i):
            @pl.when(base + i != me)
            def _():
                stats_copy(base + i).start()
                sums_copy(base + i).start()

    stats_in[me] = stats[me]
    sums_in[me] = sums[me]

    @pl.loop(1, n)
    def _(step):
        peer = me ^ step
        pltpu.make_async_remote_copy(
            src_ref=stats.at[peer], dst_ref=stats_in.at[peer], send_sem=t_send.at[peer], recv_sem=t_recv.at[peer],
            device_id={"ctx": peer}, device_id_type=MESH).wait_recv()

    st = stats_in[...].reshape(n, width)
    coef = jnp.exp2((st - jnp.max(st, axis=0, keepdims=True)) * factor) * pltpu.roll(st, width - heads, 1)
    w = coef / jnp.sum(coef, axis=0, keepdims=True)
    if n < width:
        w = jnp.concatenate([w, jnp.zeros((width - n, width), jnp.float32)], axis=0)
    w = w.T

    @pl.loop(1, n)
    def _(step):
        peer = me ^ step
        pltpu.make_async_remote_copy(
            src_ref=sums.at[peer], dst_ref=sums_in.at[peer], send_sem=s_send.at[peer], recv_sem=s_recv.at[peer],
            device_id={"ctx": peer}, device_id_type=MESH).wait_recv()

    result = jnp.zeros((heads, width), jnp.float32)
    for b in range(n):
        result += w[:heads, b:b + 1] * sums_in[b].astype(jnp.float32)
    out_ref[...] = result.astype(jnp.bfloat16)

    @pl.loop(1, n)
    def _(step):
        peer = me ^ step
        stats_copy(peer).wait_send()
        sums_copy(peer).wait_send()
        q_copy(me, peer).wait_send()


def body(n, queries, fresh_keys, fresh_values, cache_keys, stored_values, cache_lengths, positions):
    rows = queries.shape[0]
    assert rows == 1
    heads = queries.shape[1] // HEAD_WIDTH
    cache_rows, kv_width = cache_keys.shape
    chunk = 4
    assert n & (n - 1) == 0 and n % chunk == 0 and 2 * heads <= HEAD_WIDTH
    block = (n, heads, HEAD_WIDTH)
    operands = (queries, fresh_keys, fresh_values, cache_keys, stored_values, cache_lengths, positions)
    dma = pltpu.SemaphoreType.DMA
    out = pl.pallas_call(
        functools.partial(kernel, n, chunk),
        out_shape=jax.ShapeDtypeStruct((heads, HEAD_WIDTH), jnp.bfloat16),
        in_specs=[pl.BlockSpec(memory_space=pl.ANY)] * len(operands),
        out_specs=pl.BlockSpec(memory_space=pltpu.VMEM),
        scratch_shapes=[
            pltpu.VMEM((cache_rows, kv_width), jnp.bfloat16),
            pltpu.VMEM((cache_rows, kv_width), jnp.bfloat16),
            pltpu.VMEM(queries.shape, jnp.bfloat16),
            pltpu.VMEM(fresh_keys.shape, jnp.bfloat16),
            pltpu.VMEM(fresh_values.shape, jnp.bfloat16),
            pltpu.SMEM(cache_lengths.shape, jnp.int32),
            pltpu.SMEM(positions.shape, jnp.int32),
            pltpu.VMEM(block, jnp.bfloat16),
            pltpu.VMEM(block, jnp.bfloat16),
            pltpu.VMEM((n, 1, HEAD_WIDTH), jnp.float32),
            pltpu.VMEM(block, jnp.bfloat16),
            pltpu.VMEM((n, 1, HEAD_WIDTH), jnp.float32),
            dma((len(operands),)), dma((n,)), dma((n,)), dma((n,)), dma((n,)), dma((n,)), dma((n,)),
        ],
        compiler_params=pltpu.CompilerParams(collective_id=0, has_side_effects=True),
    )(*operands)
    return out.reshape(rows, heads * HEAD_WIDTH)


def solution(mesh):
    return jax.shard_map(
        functools.partial(body, mesh.shape["ctx"]),
        mesh=mesh,
        in_specs=(
            P(("groups", "ctx"), None),
            P(("groups", "ctx"), None),
            P(("groups", "ctx"), None),
            P(("groups", "ctx"), None),
            P(("groups", "ctx"), None),
            P(("groups", "ctx")),
            P("groups"),
        ),
        out_specs=P(("groups", "ctx"), None),
        check_vma=False,
    )
```

```python
import functools
import math

import jax
import jax.numpy as jnp
from jax import lax
from jax.experimental import pallas as pl
from jax.experimental.pallas import tpu as pltpu
from jax.sharding import PartitionSpec as P

HEADS_PER_GROUP = 16
HEAD_WIDTH = 128
MESH = pl.DeviceIdType.MESH


def kernel(n, chunk, queries_hbm, fresh_keys_hbm, fresh_values_hbm, keys_hbm, values_hbm, lengths_hbm, positions_hbm,
           out_ref, keys, values, q_row, fk_ref, fv_ref, lengths_ref, positions_ref,
           q_all, sums, stats, sums_in, stats_in,
           load_sem, q_send, q_recv, s_send, s_recv, t_send, t_recv):
    me = lax.axis_index("ctx")
    cache_rows = keys.shape[0]
    heads = q_all.shape[1]
    width = HEAD_WIDTH
    group = HEADS_PER_GROUP
    kv_heads = heads // group
    factor = width ** -0.5 * math.log2(math.e)
    line = n // chunk

    loads = [
        pltpu.make_async_copy(src, dst, load_sem.at[i])
        for i, (src, dst) in enumerate([
            (queries_hbm, q_row), (keys_hbm, keys), (values_hbm, values), (fresh_keys_hbm, fk_ref),
            (fresh_values_hbm, fv_ref), (lengths_hbm, lengths_ref), (positions_hbm, positions_ref)])
    ]
    for load in loads:
        load.start()

    barrier = pltpu.get_barrier_semaphore()

    @pl.loop(1, n)
    def _(step):
        pl.semaphore_signal(barrier, inc=1, device_id={"ctx": me ^ step}, device_id_type=MESH)

    loads[0].wait()
    q_all[me] = q_row[...].astype(jnp.float32).reshape(heads, width).astype(jnp.bfloat16)
    pl.semaphore_wait(barrier, n - 1)

    def q_copy(row, peer):
        return pltpu.make_async_remote_copy(
            src_ref=q_all.at[row], dst_ref=q_all.at[row], send_sem=q_send.at[0], recv_sem=q_recv.at[row],
            device_id={"ctx": peer}, device_id_type=MESH)

    @pl.loop(1, n)
    def _(step):
        q_copy(me, me ^ step).start()

    for load in loads[1:]:
        load.wait()

    dead = jnp.where(
        lax.broadcasted_iota(jnp.int32, (1, cache_rows), 1) < lengths_ref[0], 0.0, -jnp.inf
    ).astype(jnp.float32)
    lane = lax.broadcasted_iota(jnp.int32, (group, width), 1)
    row = lax.broadcasted_iota(jnp.int32, (group, width), 0)
    ones = jnp.ones((cache_rows, width), jnp.bfloat16)
    own_order = positions_ref[me]

    def sums_copy(peer):
        return pltpu.make_async_remote_copy(
            src_ref=sums.at[peer], dst_ref=sums_in.at[me], send_sem=s_send.at[0], recv_sem=s_recv.at[0],
            device_id={"ctx": peer}, device_id_type=MESH)

    def stats_copy(peer):
        return pltpu.make_async_remote_copy(
            src_ref=stats.at[peer], dst_ref=stats_in.at[me], send_sem=t_send.at[0], recv_sem=t_recv.at[0],
            device_id={"ctx": peer}, device_id_type=MESH)

    def process(base):
        fresh_bias = jnp.concatenate(
            [jnp.full((group, 1), jnp.where(own_order <= positions_ref[base + i], 0.0, -jnp.inf), jnp.float32)
             for i in range(chunk)], axis=0)
        packed = [jnp.zeros((group, width), jnp.float32) for _ in range(chunk)]
        for h in range(kv_heads):
            cols = slice(h * width, (h + 1) * width)
            q = q_all[pl.ds(base, chunk), h * group:(h + 1) * group, :].reshape(chunk * group, width)
            s = lax.dot_general(q, keys[:, cols], (((1,), (1,)), ((), ())),
                                preferred_element_type=jnp.float32) + dead
            fk = fk_ref[:, cols].astype(jnp.float32)
            fv = fv_ref[:, cols].astype(jnp.float32)
            sf = jnp.sum(q.astype(jnp.float32) * fk, axis=1, keepdims=True) + fresh_bias
            m = jnp.maximum(jnp.max(s, axis=1, keepdims=True), sf)
            p = jnp.exp2((s - m) * factor).astype(jnp.bfloat16)
            pf = jnp.exp2((sf - m) * factor).astype(jnp.bfloat16).astype(jnp.float32)
            o = jnp.dot(p, jnp.concatenate([values[:, cols], ones], axis=1), preferred_element_type=jnp.float32)
            total = o[:, width:] + pf
            block = (o[:, :width] + pf * fv) / total
            sums[pl.ds(base, chunk), h * group:(h + 1) * group, :] = block.astype(jnp.bfloat16).reshape(
                chunk, group, width)
            for i in range(chunk):
                part = slice(i * group, (i + 1) * group)
                packed[i] = jnp.where(lane == row + h * group, m[part], packed[i])
                packed[i] = jnp.where(lane == row + h * group + heads, total[part], packed[i])
        for i in range(chunk):
            stats[base + i] = jnp.sum(packed[i], axis=0, keepdims=True)

    @pl.loop(0, line)
    def _(step):
        base = (me ^ (step * chunk)) // chunk * chunk

        @pl.loop(0, chunk)
        def _(i):
            @pl.when(base + i != me)
            def _():
                q_copy(base + i, base + i).wait_recv()

        process(base)

        @pl.loop(0, chunk)
        def _(i):
            @pl.when(base + i != me)
            def _():
                stats_copy(base + i).start()
                sums_copy(base + i).start()

    stats_in[me] = stats[me]
    sums_in[me] = sums[me]

    others = pl.ds(0, n - 1)

    def all_of(src, dst, send, recv):
        return pltpu.make_async_remote_copy(
            src_ref=src.at[others], dst_ref=dst.at[others], send_sem=send.at[0], recv_sem=recv.at[0],
            device_id={"ctx": me ^ 1}, device_id_type=MESH)

    all_of(stats, stats_in, t_send, t_recv).wait_recv()

    st = stats_in[...].reshape(n, width)
    coef = jnp.exp2((st - jnp.max(st, axis=0, keepdims=True)) * factor) * pltpu.roll(st, width - heads, 1)
    w = coef / jnp.sum(coef, axis=0, keepdims=True)
    if n < width:
        w = jnp.concatenate([w, jnp.zeros((width - n, width), jnp.float32)], axis=0)
    w = w.T

    all_of(sums, sums_in, s_send, s_recv).wait_recv()

    result = jnp.zeros((heads, width), jnp.float32)
    for b in range(n):
        result += w[:heads, b:b + 1] * sums_in[b].astype(jnp.float32)
    out_ref[...] = result.astype(jnp.bfloat16)

    all_of(stats, stats_in, t_send, t_recv).wait_send()
    all_of(sums, sums_in, s_send, s_recv).wait_send()
    all_of(q_all, q_all, q_send, q_recv).wait_send()


def body(n, queries, fresh_keys, fresh_values, cache_keys, stored_values, cache_lengths, positions):
    rows = queries.shape[0]
    assert rows == 1
    heads = queries.shape[1] // HEAD_WIDTH
    cache_rows, kv_width = cache_keys.shape
    chunk = 4
    assert n & (n - 1) == 0 and n % chunk == 0 and 2 * heads <= HEAD_WIDTH
    block = (n, heads, HEAD_WIDTH)
    operands = (queries, fresh_keys, fresh_values, cache_keys, stored_values, cache_lengths, positions)
    dma = pltpu.SemaphoreType.DMA
    out = pl.pallas_call(
        functools.partial(kernel, n, chunk),
        out_shape=jax.ShapeDtypeStruct((heads, HEAD_WIDTH), jnp.bfloat16),
        in_specs=[pl.BlockSpec(memory_space=pl.ANY)] * len(operands),
        out_specs=pl.BlockSpec(memory_space=pltpu.VMEM),
        scratch_shapes=[
            pltpu.VMEM((cache_rows, kv_width), jnp.bfloat16),
            pltpu.VMEM((cache_rows, kv_width), jnp.bfloat16),
            pltpu.VMEM(queries.shape, jnp.bfloat16),
            pltpu.VMEM(fresh_keys.shape, jnp.bfloat16),
            pltpu.VMEM(fresh_values.shape, jnp.bfloat16),
            pltpu.SMEM(cache_lengths.shape, jnp.int32),
            pltpu.SMEM(positions.shape, jnp.int32),
            pltpu.VMEM(block, jnp.bfloat16),
            pltpu.VMEM(block, jnp.bfloat16),
            pltpu.VMEM((n, 1, HEAD_WIDTH), jnp.float32),
            pltpu.VMEM(block, jnp.bfloat16),
            pltpu.VMEM((n, 1, HEAD_WIDTH), jnp.float32),
            dma((len(operands),)), dma((1,)), dma((n,)), dma((1,)), dma((1,)), dma((1,)), dma((1,)),
        ],
        compiler_params=pltpu.CompilerParams(collective_id=0, has_side_effects=True),
    )(*operands)
    return out.reshape(rows, heads * HEAD_WIDTH)


def solution(mesh):
    return jax.shard_map(
        functools.partial(body, mesh.shape["ctx"]),
        mesh=mesh,
        in_specs=(
            P(("groups", "ctx"), None),
            P(("groups", "ctx"), None),
            P(("groups", "ctx"), None),
            P(("groups", "ctx"), None),
            P(("groups", "ctx"), None),
            P(("groups", "ctx")),
            P("groups"),
        ),
        out_specs=P(("groups", "ctx"), None),
        check_vma=False,
    )
```
